128 devices in a mesh: seq: 16 (over z_hi, y, core), tensor: 8 (over z_lo, x).
Axes of the slice: x: 4, y: 4, z: 4 (z_hi: 2, z_lo: 2; z = z_hi * 2 + z_lo), core: 2. Of those that a mesh axis runs over, the one named last changes fastest.
Arguments:
- tokens: bfloat16 [6144, 8192], P('seq', 'tensor'), may hold values from -6 to 6
- norm_gain: bfloat16 [8192], replicated, may hold values from 0.5 to 1.5
- w_query: bfloat16 [8192, 8192], P('seq', 'tensor')
- w_key: bfloat16 [8192, 1024], P('seq', 'tensor')
- w_value: bfloat16 [8192, 1024], P('seq', 'tensor'), may hold values from -0.1875 to 0.1875
- key_pages: bfloat16 [144, 128, 1024], P('seq', None, 'tensor'), may hold values from -15 to 15
- value_pages: bfloat16 [144, 128, 1024], P('seq', None, 'tensor'), may hold values from -16 to 16
- page_table: int32 [2, 88], replicated, may hold values from 0 to 143, as said below
- ctx_pages: int32 [2], replicated, may hold values from 1 to 64, as said below
Outputs:
- attended: bfloat16 [6144, 8192], P('seq', 'tensor')
- key_pages_out: bfloat16 [144, 128, 1024], P('seq', None, 'tensor')
- value_pages_out: bfloat16 [144, 128, 1024], P('seq', None, 'tensor')
The draws below stay inside these ranges and needn't reach their ends.
Inputs may be any that keep to these rules, and one draw needn't show every extreme that they name: `page_table`: row b lists the pool pages of sequence b: entries 0 to ctx_pages[b] - 1 hold its cached tokens, the next 24 are the pages that receive its new tokens, the rest are 0 and unused. Used entries are distinct, except that the first pages of the shorter sequence may be the first pages of the longer one (a shared prefix); pages that receive new tokens are shared with nothing. `ctx_pages`: one sequence has exactly 64 cached pages, the other fewer.
All inputs are finite; a program needn't handle non-finite values.
Results may differ from the reference program's by a relative error of at most 0.012.
The reference program's roundings to bfloat16 on the way count: a program that leaves them out, or rounds other values in their place, can miss the bound.
Values may be sent and summed in bfloat16 or wider, within the bound.
No kernel may reach another device: no remote copies, remote signals or barrier semaphores. Data moves between devices by JAX's collectives and lax.ppermute only.
A program may use at most 128 MiB of HBM per device.

```python
import math
import jax
import jax.numpy as jnp
from jax import lax

D = 8192
QH = 64
KVH = 8
HD = 128
PAGE = 128
TOKENS = 6144
SPAN = 3072
NEWP = 24
MAXCTX = 64
SHORTMAX = 16
POOL = 144


def layout_tables(key):
    base = jax.random.fold_in(key, 11)
    key_first, key_short, key_share, key_order = jax.random.split(base, 4)
    longer = jax.random.randint(key_first, (), 0, 2)
    shorter_len = jax.random.randint(key_short, (), 1, SHORTMAX + 1)
    shared = jax.random.randint(key_share, (), 0, shorter_len + 1)
    ordering = jax.random.permutation(key_order, POOL)
    leading = ordering[0]
    ordering = jnp.where(ordering == POOL - 1, leading, ordering)
    ordering = ordering.at[0].set(POOL - 1)
    width_all = MAXCTX + NEWP
    slots = jnp.arange(width_all)
    long_row = ordering[:width_all]
    picked = jnp.where(slots < shared, slots, width_all + slots - shared)
    picked = jnp.minimum(picked, POOL - 1)
    short_row = jnp.where(slots < shorter_len + NEWP, ordering[picked], 0)
    table = jnp.where(longer == 0, jnp.stack([long_row, short_row]), jnp.stack([short_row, long_row]))
    lengths = jnp.where(longer == 0, jnp.stack([jnp.int32(MAXCTX), shorter_len]), jnp.stack([shorter_len, jnp.int32(MAXCTX)]))
    return (table.astype(jnp.int32), lengths.astype(jnp.int32))


def draw_page_table(key, part):
    return layout_tables(key)[0]


def draw_ctx_pages(key, part):
    return layout_tables(key)[1]


def draw_w_key(key, part):
    base = jax.random.fold_in(key, 23)
    result = jax.random.normal(base, (D, KVH * HD), jnp.float32) * (2.5 / math.sqrt(D))
    return result.astype(jnp.bfloat16)


def draw_w_query(key, part):
    base = jax.random.fold_in(key, 29)
    key_drawn = jax.random.fold_in(base, 0)
    drawn_query = jax.random.normal(key_drawn, (D, QH * HD), jnp.float32) * (1.0 / math.sqrt(D))
    result = drawn_query
    return result.astype(jnp.bfloat16)


def draw_key_pages(key, part):
    base = jax.random.fold_in(key, 53)
    key_drawn = jax.random.fold_in(base, 0)
    drawn = jax.random.truncated_normal(key_drawn, -6.0, 6.0, (POOL, PAGE, KVH * HD), jnp.float32) * 2.5
    result = drawn
    return result.astype(jnp.bfloat16)


def steps_of(rng, dims, cuts, least, top_value):
    def one(position, shards_of):
        draws = jax.random.uniform(jax.random.fold_in(jax.random.fold_in(rng, 6), position), (shards_of,), jnp.float32, least / len(cuts), top_value / len(cuts))
        return jnp.repeat(jnp.exp(draws), dims[position] // shards_of).reshape((-1,) + (1,) * (len(dims) - position - 1))

    factor_of = one(*cuts[0])
    for cut in cuts[1:]:
        factor_of = factor_of * one(*cut)
    return factor_of


def noise(key, shape, scale, limit, pieces=(), dtype=jnp.bfloat16):
    entries = scale * jax.random.normal(key, shape, jnp.float32)
    if pieces:
        entries = entries * steps_of(key, shape, pieces, -0.22, 0.18)
    return jnp.clip(entries, -limit, limit).astype(dtype)


def setup_inputs(seed: int = 0) -> dict:
    arg_keys = jax.random.split(jax.random.key(seed), 10)
    tokens = noise(arg_keys[0], (TOKENS, D), 1.0, 6.0, ((0, 16), (1, 8)))
    norm_gain = jnp.clip(1.0 + 0.1 * jax.random.normal(arg_keys[1], (D,), jnp.float32), 0.5, 1.5).astype(jnp.bfloat16)
    w_query = draw_w_query(jax.random.fold_in(arg_keys[9], 71), 0)
    w_key = draw_w_key(jax.random.fold_in(arg_keys[9], 71), 0)
    w_value = noise(arg_keys[4], (D, KVH * HD), (D // 9) ** -0.5, 0.1875, ((0, 16), (1, 8)))
    key_pages = draw_key_pages(jax.random.fold_in(arg_keys[9], 71), 0)
    value_pages = noise(arg_keys[6], (POOL, PAGE, KVH * HD), 3.0, 16.0, ((0, 16), (2, 8)))
    page_table = draw_page_table(jax.random.fold_in(arg_keys[9], 71), 0)
    ctx_pages = draw_ctx_pages(jax.random.fold_in(arg_keys[9], 71), 0)
    return {"tokens": tokens, "norm_gain": norm_gain, "w_query": w_query, "w_key": w_key, "w_value": w_value, "key_pages": key_pages, "value_pages": value_pages, "page_table": page_table, "ctx_pages": ctx_pages}


def reference(tokens, norm_gain, w_query, w_key, w_value, key_pages, value_pages, page_table, ctx_pages):
    widened = tokens.astype(jnp.float32)
    normed = (widened * lax.rsqrt(lax.optimization_barrier(jnp.mean(widened * widened, -1, keepdims=True)) + 1e-05) * norm_gain.astype(jnp.float32)).astype(jnp.bfloat16)
    queries = jnp.dot(normed, w_query, preferred_element_type=jnp.float32).astype(jnp.bfloat16)
    keys_new = jnp.dot(normed, w_key, preferred_element_type=jnp.float32).astype(jnp.bfloat16)
    values_new = jnp.dot(normed, w_value, preferred_element_type=jnp.float32).astype(jnp.bfloat16)
    groups = QH // KVH
    score_scale = HD ** (-0.5)
    results = []
    for seq_no in range(2):
        page_rows = page_table[seq_no, :MAXCTX]
        cached_k = key_pages[page_rows].reshape(MAXCTX * PAGE, KVH, HD)
        cached_v = value_pages[page_rows].reshape(MAXCTX * PAGE, KVH, HD)
        fresh_k = keys_new[seq_no * SPAN:(seq_no + 1) * SPAN].reshape(SPAN, KVH, HD)
        fresh_v = values_new[seq_no * SPAN:(seq_no + 1) * SPAN].reshape(SPAN, KVH, HD)
        every_k = jnp.concatenate([cached_k, fresh_k], 0)
        every_v = jnp.concatenate([cached_v, fresh_v], 0)
        cached_live = jnp.arange(MAXCTX * PAGE) // PAGE < ctx_pages[seq_no]
        causal = jnp.arange(SPAN)[None, :] <= jnp.arange(SPAN)[:, None]
        visible = jnp.concatenate([jnp.broadcast_to(cached_live[None, :], (SPAN, MAXCTX * PAGE)), causal], 1)
        seq_queries = queries[seq_no * SPAN:(seq_no + 1) * SPAN].reshape(SPAN, QH, HD)

        def one_head(head_no):
            q_head = lax.dynamic_index_in_dim(seq_queries, head_no, 1, False)
            k_head = lax.dynamic_index_in_dim(every_k, head_no // groups, 1, False)
            v_head = lax.dynamic_index_in_dim(every_v, head_no // groups, 1, False)
            scores = jnp.dot(q_head, k_head.T, preferred_element_type=jnp.float32) * score_scale
            scores = jnp.where(visible, scores, -1e+30)
            maxima = lax.optimization_barrier(jnp.max(scores, -1, keepdims=True))
            raised = jnp.exp(scores - maxima)
            totals = lax.optimization_barrier(jnp.sum(raised, -1, keepdims=True))
            return jnp.dot(raised.astype(jnp.bfloat16), v_head, preferred_element_type=jnp.float32) / totals
        heads_out = lax.map(one_head, jnp.arange(QH))
        results.append(jnp.transpose(heads_out, (1, 0, 2)).reshape(SPAN, QH * HD).astype(jnp.bfloat16))
    attended = jnp.concatenate(results, 0)
    targets = jnp.concatenate([lax.dynamic_slice_in_dim(page_table[seq_no], ctx_pages[seq_no].astype(jnp.int32), NEWP, 0) for seq_no in range(2)])
    key_pages_out = key_pages.at[targets].set(keys_new.reshape(2 * NEWP, PAGE, KVH * HD))
    value_pages_out = value_pages.at[targets].set(values_new.reshape(2 * NEWP, PAGE, KVH * HD))
    return (attended, key_pages_out, value_pages_out)
```

```python
import jax
import jax.numpy as jnp
from jax import lax
from jax.experimental import pallas as pl
from jax.experimental.pallas import tpu as pltpu
from jax.sharding import PartitionSpec as P

HD = 128
PAGE = 128
ROWS = 384
HALF = 4096
SHARD = 512
NQ = 512
HEADS = 4
QR = HEADS * ROWS
POOL_LOCAL = 9
KBLK = 8
KEYS = KBLK * PAGE
RT = 256
NEG = -1e30
SCALE2 = (HD**-0.5) * 1.4426950408889634
BF = jnp.bfloat16
F32 = jnp.float32


def seq_perm(f):
    out = []
    for i in range(16):
        h, y, c = i // 8, (i // 2) % 4, i % 2
        h2, y2, c2 = f(h, y, c)
        out.append((i, (h2 % 2) * 8 + (y2 % 4) * 2 + c2 % 2))
    return out


def tensor_perm(f):
    out = []
    for t in range(8):
        l2, x2 = f(t // 4, t % 4)
        out.append((t, (l2 % 2) * 4 + x2 % 4))
    return out


Y_UP = seq_perm(lambda h, y, c: (h, y + 1, c))
Y_DOWN = seq_perm(lambda h, y, c: (h, y - 1, c))
Y_FAR = seq_perm(lambda h, y, c: (h, y + 2, c))
CORE = seq_perm(lambda h, y, c: (h, y, c + 1))
PARTNER = seq_perm(lambda h, y, c: (h + 1, y, c))
X_UP = tensor_perm(lambda l, x: (l, x + 1))
X_DOWN = tensor_perm(lambda l, x: (l, x - 1))
X_FAR = tensor_perm(lambda l, x: (l, x + 2))
Z_LOW = tensor_perm(lambda l, x: (l + 1, x))


def z_perm(moves):
    out = []
    for s in range(16):
        for t in range(8):
            h, l = s // 8, t // 4
            z = h * 2 + l
            if z in moves:
                z2 = moves[z]
                s2 = (z2 // 2) * 8 + s % 8
                t2 = (z2 % 2) * 4 + t % 4
                out.append((s * 8 + t, s2 * 8 + t2))
    return out


Z_FIRST = z_perm({0: 1, 3: 2, 1: 3, 2: 0})
Z_SECOND = z_perm({2: 1, 1: 2})

ANY = pl.BlockSpec(memory_space=pl.ANY)
FULL = pl.BlockSpec(memory_space=pltpu.VMEM)


def copy_all(copies):
    for cp in copies:
        cp.start()
    for cp in copies:
        cp.wait()


def proj_kernel(meta, *refs):
    xs_in = refs[0:8]
    ws_in = refs[8:18]
    scale, gain = refs[18:20]
    qm, qt, kvf, kvb = refs[20:24]
    xv, wv, sems = refs[24:27]
    x, y, c, h = meta[0], meta[1], meta[2], meta[3]
    copies = []
    for k, shift in enumerate((0, 3, 1, 2)):
        xa = lax.rem(x + shift, 4)
        for half in range(2):
            copies.append(
                pltpu.make_async_copy(
                    xs_in[2 * k + half],
                    xv.at[pl.ds(half * ROWS, ROWS), pl.ds(pl.multiple_of(xa * 1024, 1024), 1024)],
                    sems.at[len(copies)],
                )
            )
    for side in range(2):
        cc = c if side == 0 else 1 - c
        for k, shift in enumerate((0, 3, 1)):
            row = pl.multiple_of((lax.rem(y + shift, 4) * 2 + cc) * SHARD, SHARD)
            copies.append(
                pltpu.make_async_copy(
                    ws_in[5 * side + k], wv.at[pl.ds(row, SHARD), :], sems.at[len(copies)]
                )
            )
        for k in range(2):
            row = pl.multiple_of(
                (lax.rem(y + 2, 4) * 2 + cc) * SHARD + k * (SHARD // 2), SHARD // 2
            )
            copies.append(
                pltpu.make_async_copy(
                    ws_in[5 * side + 3 + k],
                    wv.at[pl.ds(row, SHARD // 2), :],
                    sems.at[len(copies)],
                )
            )
    copy_all(copies)

    def norm_step(r, carry):
        row = pl.multiple_of(r * 16, 16)
        wide = xv[pl.ds(row, 16), :].astype(F32)
        factor = lax.rsqrt(scale[pl.ds(row, 16), :] * (1.0 / 8192.0) + 1e-05)
        xv[pl.ds(row, 16), :] = (wide * factor * gain[...]).astype(BF)
        return carry

    lax.fori_loop(0, 2 * ROWS // 16, norm_step, 0)

    def product(col):
        return jnp.dot(xv[...], wv[:, pl.ds(col, 256)], preferred_element_type=F32)

    kv = product(1024)
    kvf[...] = kv
    kvb[...] = kv.astype(BF)
    for n in range(2):
        qm[:, n * 256 : (n + 1) * 256] = product(pl.multiple_of(h * NQ + n * 256, 256))
        qt[:, n * 256 : (n + 1) * 256] = product(
            pl.multiple_of((1 - h) * NQ + n * 256, 256)
        ).astype(BF)


def flash_step(s, m_ref, acc_ref, i, row, rows, values):
    m_old = m_ref[i, pl.ds(row, rows), :]
    m_new = jnp.maximum(m_old, jnp.max(s, -1, keepdims=True))
    p = jnp.exp2(s - m_new).astype(BF)
    shrink = jnp.exp2(m_old - m_new)
    acc_ref[i, pl.ds(row, rows), :] = acc_ref[i, pl.ds(row, rows), :] * shrink + jnp.dot(
        p, values, preferred_element_type=F32
    )
    m_ref[i, pl.ds(row, rows), :] = m_new


def scores_of(q, k):
    return (
        lax.dot_general(q, k, (((1,), (1,)), ((), ())), preferred_element_type=F32) * SCALE2
    )


def cached_kernel(meta, table, ctx, qm, qr, pool, q_out, acc, m, kbuf, vbuf, sems):
    l = meta[4]
    for i in range(2):
        for hd in range(HEADS):
            rows = slice(i * ROWS, (i + 1) * ROWS)
            cols = slice(hd * HD, (hd + 1) * HD)
            q_out[i, hd * ROWS : (hd + 1) * ROWS, :] = (
                qm[rows, cols] + qr[rows, cols].astype(F32)
            ).astype(BF)
    m[...] = jnp.full_like(m, NEG)
    acc[...] = jnp.zeros_like(acc)
    vbuf[:, :, HD:] = jnp.ones((2, KEYS, HD), BF)
    n0 = ctx[1 - l]
    n1 = ctx[l]
    blocks0 = lax.div(n0 + KBLK - 1, KBLK)
    blocks1 = lax.div(n1 + KBLK - 1, KBLK)
    total = blocks0 + blocks1

    def place(t):
        second = t >= blocks0
        i = second.astype(jnp.int32)
        blk = jnp.where(second, t - blocks0, t)
        return i, blk

    def copies_of(t, slot):
        i, blk = place(t)
        b = jnp.where(i == 0, 1 - l, l)
        n = jnp.where(i == 0, n0, n1)
        out = []
        for j in range(KBLK):
            g = table[b, jnp.minimum(blk * KBLK + j, n - 1)]
            owner = lax.div(g, POOL_LOCAL)
            local = lax.rem(g, POOL_LOCAL)
            out.append(
                pltpu.make_async_copy(
                    pool.at[owner, 0, local],
                    kbuf.at[slot, pl.ds(j * PAGE, PAGE), :],
                    sems.at[slot, 0, j],
                )
            )
            out.append(
                pltpu.make_async_copy(
                    pool.at[owner, 1, local],
                    vbuf.at[slot, pl.ds(j * PAGE, PAGE), pl.ds(0, HD)],
                    sems.at[slot, 1, j],
                )
            )
        return out

    for cp in copies_of(0, 0):
        cp.start()

    def block_step(t, carry):
        slot = lax.rem(t, 2)
        for cp in copies_of(t, slot):
            cp.wait()

        @pl.when(t + 1 < total)
        def _():
            for cp in copies_of(t + 1, 1 - slot):
                cp.start()

        i, blk = place(t)
        n = jnp.where(i == 0, n0, n1)
        live = (n - blk * KBLK) * PAGE

        def rows_step(r, carry, masked):
            row = pl.multiple_of(r * RT, RT)
            s = scores_of(q_out[i, pl.ds(row, RT), :], kbuf[slot])
            if masked:
                s = jnp.where(lax.broadcasted_iota(jnp.int32, s.shape, 1) < live, s, NEG)
            flash_step(s, m, acc, i, row, RT, vbuf[slot])
            return carry

        @pl.when(live >= KEYS)
        def _():
            lax.fori_loop(0, QR // RT, lambda r, cc: rows_step(r, cc, False), 0, unroll=2)

        @pl.when(live < KEYS)
        def _():
            lax.fori_loop(0, QR // RT, lambda r, cc: rows_step(r, cc, True), 0)

        return carry

    lax.fori_loop(0, total, block_step, 0)


def fresh_copies(meta, i, kv_refs, kbuf, vbuf, sems):
    y, c = meta[1], meta[2]
    own, swapped, others, others_swapped = kv_refs
    out = []
    for side in range(2):
        cc = c if side == 0 else 1 - c
        for k, shift in enumerate((0, 3, 1, 2)):
            place = lax.rem(y + shift, 4) * 2 + cc
            src = (own, swapped)[side] if k == 0 else (others, others_swapped)[side].at[k - 1]
            rows = pl.ds(pl.multiple_of(i * ROWS, ROWS), ROWS)
            dst = pl.ds(pl.multiple_of(place * ROWS, ROWS), ROWS)
            n = len(out)
            out.append(
                pltpu.make_async_copy(
                    src.at[rows, pl.ds(0, HD)], kbuf.at[dst, :], sems.at[n]
                )
            )
            out.append(
                pltpu.make_async_copy(
                    src.at[rows, pl.ds(HD, HD)], vbuf.at[dst, pl.ds(0, HD)], sems.at[n + 1]
                )
            )
    return out


def causal_body(meta, q, acc_in, m_in, out, kbuf, vbuf, acc, m):
    p_own = meta[1] * 2 + meta[2]
    acc[...] = acc_in[...]
    m[...] = m_in[...]

    def block_step(pb, carry):
        at = pl.ds(pl.multiple_of(pb * ROWS, ROWS), ROWS)

        def head_step(hd, carry):
            row = pl.multiple_of(hd * ROWS, ROWS)
            s = scores_of(q[0, pl.ds(row, ROWS), :], kbuf[at, :])
            flash_step(s, m, acc, 0, row, ROWS, vbuf[at, :])
            return carry

        return lax.fori_loop(0, HEADS, head_step, carry, unroll=2)

    lax.fori_loop(0, p_own, block_step, 0)
    at = pl.ds(pl.multiple_of(p_own * ROWS, ROWS), ROWS)
    seen = lax.broadcasted_iota(jnp.int32, (ROWS, ROWS), 1) <= lax.broadcasted_iota(
        jnp.int32, (ROWS, ROWS), 0
    )
    for hd in range(HEADS):
        row = hd * ROWS
        s = jnp.where(seen, scores_of(q[0, row : row + ROWS, :], kbuf[at, :]), NEG)
        flash_step(s, m, acc, 0, row, ROWS, vbuf[at, :])
        out[:, hd * HD : (hd + 1) * HD] = (
            acc[0, row : row + ROWS, :HD] / acc[0, row : row + ROWS, HD:]
        ).astype(BF)


def causal_kernel(meta, src, q, acc_in, m_in, *refs, with_pages, which):
    kv_refs = refs[:4]
    if with_pages:
        kp, vp, out, kp_out, vp_out = refs[4:9]
        kbuf, vbuf, acc, m, sems, page_sems = refs[9:]
    else:
        out, kbuf, vbuf, acc, m, sems = refs[4:]
    y, c, l = meta[1], meta[2], meta[4]
    i = meta[5 + which]
    copies = fresh_copies(meta, i, kv_refs, kbuf, vbuf, sems)
    for cp in copies:
        cp.start()
    vbuf[:, HD:] = jnp.ones((2 * 4 * ROWS, HD), BF)
    if with_pages:
        own, swapped, others, others_swapped = kv_refs

        def page_copy(n, run):
            def put(ksrc, vsrc):
                for cp in (
                    pltpu.make_async_copy(ksrc, kp_out.at[n], page_sems.at[0, n]),
                    pltpu.make_async_copy(vsrc, vp_out.at[n], page_sems.at[1, n]),
                ):
                    run(cp)

            which_new = src[n]

            @pl.when(which_new < 0)
            def _():
                put(kp.at[n], vp.at[n])

            new = jnp.maximum(which_new, 0)
            b = lax.div(new, 24)
            j = lax.rem(new, 24)
            place = lax.div(j, 3)
            half = jnp.where(b == l, 1, 0)
            row = pl.multiple_of(half * ROWS + lax.rem(j, 3) * PAGE, PAGE)
            rows = pl.ds(row, PAGE)
            step = lax.rem(lax.div(place, 2) - y + 4, 4)
            same = lax.rem(place, 2) == c
            entry = jnp.where(step == 3, 0, jnp.where(step == 1, 1, 2))
            fresh = which_new >= 0
            for is_same in (True, False):
                core_ok = same if is_same else jnp.logical_not(same)
                near = own if is_same else swapped
                far = others if is_same else others_swapped

                @pl.when(fresh & core_ok & (step == 0))
                def _():
                    put(near.at[rows, pl.ds(0, HD)], near.at[rows, pl.ds(HD, HD)])

                @pl.when(fresh & core_ok & (step != 0))
                def _():
                    put(
                        far.at[entry, rows, pl.ds(0, HD)], far.at[entry, rows, pl.ds(HD, HD)]
                    )

        def start_page(n, carry):
            page_copy(n, lambda cp: cp.start())
            return carry

        lax.fori_loop(0, POOL_LOCAL, start_page, 0)
    for cp in copies:
        cp.wait()
    causal_body(meta, q, acc_in, m_in, out, kbuf, vbuf, acc, m)
    if with_pages:

        def wait_page(n, carry):
            for side, (a, o) in enumerate(((kp, kp_out), (vp, vp_out))):
                pltpu.make_async_copy(a.at[n], o.at[n], page_sems.at[side, n]).wait()
            return carry

        lax.fori_loop(0, POOL_LOCAL, wait_page, 0)


PARAMS = dict(vmem_limit_bytes=60 * 1024 * 1024)


def project(meta, xs, ws, scale, gain):
    return pl.pallas_call(
        proj_kernel,
        grid_spec=pltpu.PrefetchScalarGridSpec(
            num_scalar_prefetch=1,
            in_specs=[ANY] * 18 + [FULL] * 2,
            out_specs=[FULL] * 4,
            scratch_shapes=[
                pltpu.VMEM((2 * ROWS, HALF), BF),
                pltpu.VMEM((HALF, 1280), BF),
                pltpu.SemaphoreType.DMA((18,)),
            ],
        ),
        out_shape=[
            jax.ShapeDtypeStruct((2 * ROWS, NQ), F32),
            jax.ShapeDtypeStruct((2 * ROWS, NQ), BF),
            jax.ShapeDtypeStruct((2 * ROWS, 2 * HD), F32),
            jax.ShapeDtypeStruct((2 * ROWS, 2 * HD), BF),
        ],
        compiler_params=pltpu.CompilerParams(**PARAMS),
        name="project",
    )(meta, *xs, *ws, scale, gain)


def cached_attention(meta, table, ctx, qm, qr, pool):
    return pl.pallas_call(
        cached_kernel,
        grid_spec=pltpu.PrefetchScalarGridSpec(
            num_scalar_prefetch=3,
            in_specs=[FULL, FULL, ANY],
            out_specs=[FULL] * 3,
            scratch_shapes=[
                pltpu.VMEM((2, KEYS, HD), BF),
                pltpu.VMEM((2, KEYS, 2 * HD), BF),
                pltpu.SemaphoreType.DMA((2, 2, KBLK)),
            ],
        ),
        out_shape=[
            jax.ShapeDtypeStruct((2, QR, HD), BF),
            jax.ShapeDtypeStruct((2, QR, 2 * HD), F32),
            jax.ShapeDtypeStruct((2, QR, 1), F32),
        ],
        compiler_params=pltpu.CompilerParams(**PARAMS),
        name="cached",
    )(meta, table, ctx, qm, qr, pool)


def causal_attention(meta, src, q, acc, m, kv, pages, which):
    with_pages = pages is not None

    def half(d):
        return pl.BlockSpec((1, QR, d), lambda g, meta, src: (meta[5 + which], 0, 0))

    scratch = [
        pltpu.VMEM((8 * ROWS, HD), BF),
        pltpu.VMEM((8 * ROWS, 2 * HD), BF),
        pltpu.VMEM((1, QR, 2 * HD), F32),
        pltpu.VMEM((1, QR, 1), F32),
        pltpu.SemaphoreType.DMA((16,)),
    ]
    out_specs = [pl.BlockSpec((ROWS, NQ), lambda g, meta, src: (0, 0))]
    out_shape = [jax.ShapeDtypeStruct((ROWS, NQ), BF)]
    if with_pages:
        scratch.append(pltpu.SemaphoreType.DMA((2, POOL_LOCAL)))
        out_specs += [ANY, ANY]
        out_shape += [jax.ShapeDtypeStruct(p.shape, p.dtype) for p in pages]
    return pl.pallas_call(
        lambda *refs: causal_kernel(*refs, with_pages=with_pages, which=which),
        grid_spec=pltpu.PrefetchScalarGridSpec(
            num_scalar_prefetch=2,
            grid=(1,),
            in_specs=[half(HD), half(2 * HD), half(1)] + [ANY] * (4 + 2 * with_pages),
            out_specs=out_specs,
            scratch_shapes=scratch,
        ),
        out_shape=out_shape,
        compiler_params=pltpu.CompilerParams(**PARAMS),
        name="causal",
    )(meta, src, q, acc, m, *kv, *(pages if with_pages else ()))


def local(
    tokens, norm_gain, w_query, w_key, w_value, key_pages, value_pages, page_table, ctx_pages
):
    s_at = lax.axis_index("seq")
    t_at = lax.axis_index("tensor")
    h, y, c = s_at // 8, (s_at // 2) % 4, s_at % 2
    l, x = t_at // 4, t_at % 4
    own_half = jnp.where(l == h, 1, 0)
    meta = jnp.stack([x, y, c, h, l, 1 - own_half, own_half]).astype(jnp.int32)

    def over_seq(a, perm):
        return lax.ppermute(a, "seq", perm)

    def over_tensor(a, perm):
        return lax.ppermute(a, "tensor", perm)

    first = lax.ppermute(tokens, ("seq", "tensor"), Z_FIRST)
    second = lax.ppermute(tokens, ("seq", "tensor"), Z_SECOND)
    second = jnp.where(l == h, tokens, second)
    up_b, down_b = over_tensor(second, X_UP), over_tensor(second, X_DOWN)
    up_a, down_a = over_tensor(first, X_UP), over_tensor(first, X_DOWN)
    far_a = over_tensor(up_a, X_UP)
    far_b = over_tensor(down_b, X_DOWN)
    xs = (first, second, up_a, up_b, down_a, down_b, far_a, far_b)

    w_own = jnp.concatenate([w_query, w_key, w_value], 1)
    w_up, w_down = over_seq(w_own, Y_UP), over_seq(w_own, Y_DOWN)
    w_far_top = over_seq(w_up[: SHARD // 2], Y_UP)
    w_far_bottom = over_seq(w_down[SHARD // 2 :], Y_DOWN)
    w_here = (w_own, w_up, w_down, w_far_top, w_far_bottom)
    ws = w_here + tuple(over_seq(w, CORE) for w in w_here)

    wide = tokens.astype(F32)
    squares = jnp.sum(wide * wide, -1)
    squares = squares + over_tensor(squares, Z_LOW)
    squares = squares + over_tensor(squares, X_FAR)
    squares = squares + over_tensor(squares, tensor_perm(lambda l, x: (l, x ^ 1)))
    other = over_seq(squares, PARTNER)
    scale = jnp.where(
        l == h, jnp.concatenate([other, squares]), jnp.concatenate([squares, other])
    )
    gain = lax.dynamic_slice_in_dim(norm_gain, h * HALF, HALF, 0)

    pool = lax.all_gather(jnp.stack([key_pages, value_pages]), "seq", axis=0)

    q_mine, q_theirs, kv_mine, kv_theirs = project(
        meta, xs, ws, scale.reshape(2 * ROWS, 1), gain.astype(F32).reshape(1, HALF)
    )
    kv_received = over_seq(kv_theirs, PARTNER)
    q_received = over_seq(q_theirs, PARTNER)
    kv_own = (kv_mine + kv_received.astype(F32)).astype(BF)
    kv_swapped = over_seq(kv_own, CORE)
    kv_others = jnp.stack([over_seq(kv_own, p) for p in (Y_UP, Y_DOWN, Y_FAR)])
    kv_others_swapped = over_seq(kv_others, CORE)
    kv = (kv_own, kv_swapped, kv_others, kv_others_swapped)

    q, acc, m = cached_attention(meta, page_table, ctx_pages, q_mine, q_received, pool)

    targets = jnp.concatenate(
        [lax.dynamic_slice_in_dim(page_table[b], ctx_pages[b], 24, 0) for b in range(2)]
    )
    hit = (s_at * POOL_LOCAL + jnp.arange(POOL_LOCAL))[:, None] == targets[None, :]
    src = jnp.max(jnp.where(hit, jnp.arange(48)[None, :], -1), 1).astype(jnp.int32)

    (for_partner,) = causal_attention(meta, src, q, acc, m, kv, None, 0)
    received = over_seq(for_partner, PARTNER)
    mine, key_pages_out, value_pages_out = causal_attention(
        meta, src, q, acc, m, kv, (key_pages, value_pages), 1
    )
    attended = jnp.where(
        h == 0,
        jnp.concatenate([mine, received], 1),
        jnp.concatenate([received, mine], 1),
    )
    return (attended, key_pages_out, value_pages_out)


def solution(mesh):
    return jax.shard_map(
        local,
        mesh=mesh,
        in_specs=(
            P("seq", "tensor"),
            P(),
            P("seq", "tensor"),
            P("seq", "tensor"),
            P("seq", "tensor"),
            P("seq", None, "tensor"),
            P("seq", None, "tensor"),
            P(),
            P(),
        ),
        out_specs=(P("seq", "tensor"), P("seq", None, "tensor"), P("seq", None, "tensor")),
        check_vma=False,
    )
```
